512 devices in a mesh: node: 32 (over x, y, core), mode: 16 (over z).
Axes of the slice: x: 4, y: 4, z: 16, core: 2. Of those that a mesh axis runs over, the one named last changes fastest.
Arguments:
- panels: float32 [288, 16384], P('mode', 'node'), may hold values from -6 to 6
- blocks: float32 [11, 3, 64, 16384], P(None, None, None, 'node'), may hold values from -0.4375 to 0.4375
- cols: int32 [11, 3, 256], P(None, None, 'node'), may hold values from 0 to 255, as said below
Outputs:
- result: float32 [288, 16384], P('mode', 'node')
The draws below stay inside these ranges and needn't reach their ends.
Inputs may be any that keep to these rules, and one draw needn't show every extreme that they name: cols[i, s, r] differs from r by at most 1.
All inputs are finite; a program needn't handle non-finite values.
Results may differ from the reference program's by a relative error of at most 0.0001.
Values sent between devices are 32-bit elements; how exact they have to be, the bound alone decides.
No kernel may reach another device: no remote copies, remote signals or barrier semaphores. Data moves between devices by JAX's collectives and lax.ppermute only.
A program may use at most 64 MiB of HBM per device.

```python
import math
import jax
import jax.numpy as jnp
import numpy as np
from jax import lax

MAT = 11
ORDER = 3
MODES = 288
BLOCK = 64
NNZ = 3
HALO_BLK = 1
NBLK = 256
NODES = 16384


def draw_cols(key, part):
    block_rows = jnp.arange(NBLK, dtype=jnp.int32)
    offsets = jax.random.randint(key, (MAT, NNZ, NBLK), -HALO_BLK, HALO_BLK + 1, dtype=jnp.int32)
    return jnp.clip(block_rows + offsets, 0, NBLK - 1).astype(jnp.int32)


def block_scale(key, shape, split, smallest, high):
    def one(axis_at, blocks):
        steps = jax.random.uniform(jax.random.fold_in(jax.random.fold_in(key, 6), axis_at), (blocks,), jnp.float32, smallest / len(split), high / len(split))
        return jnp.repeat(jnp.exp(steps), shape[axis_at] // blocks).reshape((-1,) + (1,) * (len(shape) - axis_at - 1))

    gain = one(*split[0])
    for cut in split[1:]:
        gain = gain * one(*cut)
    return gain


def centred(key, shape, scale, bound, split=(), kind=jnp.bfloat16):
    drawn = scale * jax.random.normal(key, shape, jnp.float32)
    if split:
        drawn = drawn * block_scale(key, shape, split, -0.22, 0.18)
    return jnp.clip(drawn, -bound, bound).astype(kind)


def setup_inputs(seed: int = 0) -> dict:
    splits = jax.random.split(jax.random.key(seed), 4)
    return {
        "panels": centred(splits[0], (MODES, NODES), 1.0, 6.0, ((0, 16), (1, 32)), jnp.float32),
        "blocks": centred(splits[1], (MAT, NNZ, BLOCK, NODES), (NNZ * BLOCK) ** -0.5, 0.4375, ((3, 32),), jnp.float32),
        "cols": draw_cols(jax.random.fold_in(splits[3], 71), 0),
    }


def degree_lists(count, total):
    if count == 1:
        return [[total]]
    collected = []
    for leading in range(total, -1, -1):
        for remainder in degree_lists(count - 1, total - leading):
            collected.append([leading] + remainder)
    return collected

def chaos_table(mat_count, mode_count, order_max):
    variables = mat_count - 1
    indices = []
    for degree in range(order_max + 1):
        indices.extend(degree_lists(variables, degree))
    indices = indices[:mode_count]
    lookup = {tuple(vector): position for position, vector in enumerate(indices)}
    table = np.zeros((mat_count, mode_count, mode_count))
    for column, vector in enumerate(indices):
        table[0, column, column] = 1.0
        for variable in range(variables):
            raised = list(vector)
            raised[variable] = raised[variable] + 1
            if tuple(raised) in lookup:
                target = lookup[tuple(raised)]
                weight_value = math.sqrt(vector[variable] + 1)
                table[variable + 1, target, column] = weight_value
                table[variable + 1, column, target] = weight_value
    return table

def reference(panels, blocks, cols):
    coupling = jnp.asarray(chaos_table(MAT, MODES, ORDER)).astype(jnp.float32)
    panel_blocks = panels.reshape(MODES, NBLK, BLOCK)
    value_blocks = blocks.reshape(MAT, NNZ, BLOCK, NBLK, BLOCK)

    def add_matrix(running, matrix_index):
        gathered = jnp.take(panel_blocks, cols[matrix_index], axis=1)
        products = jnp.einsum('sbra,jsrb->jra', value_blocks[matrix_index], gathered, precision=lax.Precision.HIGHEST)
        products = products.reshape(MODES, NODES)
        running = running + jnp.dot(coupling[matrix_index], products, precision=lax.Precision.HIGHEST, preferred_element_type=jnp.float32)
        return (running, None)
    initial = jnp.zeros((MODES, NODES), jnp.float32)
    result, unused = lax.scan(add_matrix, initial, jnp.arange(MAT, dtype=jnp.int32))
    return result
```

```python
import functools

import jax
import jax.numpy as jnp
import numpy as np
from jax import lax
from jax.experimental import pallas as pl
from jax.experimental.pallas import tpu as pltpu
from jax.sharding import PartitionSpec as P

MAT = 11
VARS = MAT - 1
ORDER = 3
MODES = 288
BLOCK = 64
NNZ = 3
DEPTH = MAT * NNZ * BLOCK
GROUPS = 16
OWN = MODES // GROUPS
ROWS = 8
SLOTS = 10
WIDTH = SLOTS * BLOCK
PAD = 32
STEP = 24
LANES = 128
PAIRS = 17


def degree_lists(count, total):
    if count == 1:
        return [[total]]
    collected = []
    for leading in range(total, -1, -1):
        for remainder in degree_lists(count - 1, total - leading):
            collected.append([leading] + remainder)
    return collected


def mode_tables():
    indices = []
    for degree in range(ORDER + 1):
        indices.extend(degree_lists(VARS, degree))
    indices = indices[:MODES]
    own = np.full((GROUPS, PAD, LANES), -100.0, np.float32)
    every = np.full((16, GROUPS * STEP), 100.0, np.float32)
    for mode, vector in enumerate(indices):
        group, row = divmod(mode, OWN)
        own[group, row, :VARS] = vector
        every[:VARS, group * STEP + row] = vector
    return own, every


def split(value):
    high = value.astype(jnp.bfloat16)
    return high, (value - high.astype(jnp.float32)).astype(jnp.bfloat16)


def kernel(cols_ref, own_tab, every_tab, x_ref, gathered_ref, blocks_ref, out_ref,
           panel, coup, mixed_hi, mixed_lo, lhs, low):
    group = lax.axis_index("mode")
    first = lax.axis_index("node") * ROWS
    lane = lax.broadcasted_iota(jnp.int32, (PAD, LANES), 1)
    left = lane < BLOCK

    for g in range(GROUPS):
        rows = jnp.concatenate([gathered_ref[g], jnp.zeros((STEP - OWN, WIDTH), jnp.float32)], axis=0)
        panel[pl.ds(g * STEP, STEP), :] = rows

    own = own_tab[group]
    every = every_tab[...]
    gaps = [own[:, p : p + 1] - every[p : p + 1, :] for p in range(VARS)]
    apart = functools.reduce(lambda a, b: a + b, [g * g for g in gaps])
    adjacent = apart == 1.0
    for p in range(VARS):
        top = jnp.maximum(own[:, p : p + 1], every[p : p + 1, :])
        root = jnp.where(top == 1.0, 1.0, jnp.where(top == 2.0, np.float32(2.0**0.5), np.float32(3.0**0.5)))
        c_hi, c_lo = split(jnp.where(adjacent & (gaps[p] != 0.0), root, 0.0))
        coup[pl.ds(p * PAD, PAD), :] = c_hi
        coup[pl.ds((VARS + p) * PAD, PAD), :] = c_lo

    def keep(i, c, value):
        turned = pltpu.roll(value, BLOCK, 1)
        for half in range(2):
            pick = jnp.where(left, value, turned) if half == 0 else jnp.where(left, turned, value)
            hi, lo = split(pick)
            mixed_hi[i, 2 * c + half] = hi
            mixed_lo[i, 2 * c + half] = lo

    valid = own[:, 0:1] >= 0.0
    for c in range(WIDTH // LANES):
        at = pl.ds(c * LANES, LANES)
        mine = jnp.concatenate([x_ref[:, at], jnp.zeros((PAD - OWN, LANES), jnp.float32)], axis=0)
        keep(0, c, jnp.where(valid, mine, 0.0))
    half = VARS * PAD
    for c0, cw in ((0, 256), (256, 256), (512, 128)):
        p_hi, p_lo = split(panel[:, c0 : c0 + cw])
        both = jnp.dot(coup[...], p_hi, preferred_element_type=jnp.float32)
        mixed = both[:half] + both[half:] + jnp.dot(coup[:half], p_lo, preferred_element_type=jnp.float32)
        for p in range(VARS):
            for c in range(cw // LANES):
                keep(p + 1, c0 // LANES + c, mixed[p * PAD : (p + 1) * PAD, c * LANES : (c + 1) * LANES])

    def slot(i, s, r):
        rel = cols_ref[i, s, r] - first
        return jnp.where(rel < 0, ROWS, jnp.where(rel == ROWS, ROWS + 1, rel))

    for r in range(ROWS):
        for q in range(PAIRS):
            ia, sa = divmod(2 * q, NNZ)
            a = slot(ia, sa, r)
            at = pl.ds(q * LANES, LANES)
            if 2 * q + 1 < MAT * NNZ:
                ib, sb = divmod(2 * q + 1, NNZ)
                b = slot(ib, sb, r)
                hi = jnp.where(left, mixed_hi[ia, a], mixed_hi[ib, b])
                lo = jnp.where(left, mixed_lo[ia, a], mixed_lo[ib, b])
            else:
                hi, lo = mixed_hi[ia, a], mixed_lo[ia, a]
            lhs[r // 4, pl.ds((r % 4) * PAD, PAD), at] = hi
            lhs[r // 4, pl.ds((4 + r % 4) * PAD, PAD), at] = lo

    for t in range(2):
        total = None
        for k0, kw in ((0, 512), (512, 512), (1024, 512), (1536, 576)):
            w_hi, w_lo = split(blocks_ref[pl.ds(k0, kw), pl.ds(t * 256, 256)])
            both = jnp.dot(lhs[t, :, k0 : k0 + kw], w_hi, preferred_element_type=jnp.float32)
            part = both[: 4 * PAD] + both[4 * PAD :]
            part = part + jnp.dot(lhs[t, : 4 * PAD, k0 : k0 + kw], w_lo, preferred_element_type=jnp.float32)
            total = part if total is None else total + part
        for h in range(2):
            cut = total[:, h * LANES : (h + 1) * LANES]
            one, two = cut[(2 * h) * PAD : (2 * h + 1) * PAD], cut[(2 * h + 1) * PAD : (2 * h + 2) * PAD]
            out_ref[:, pl.ds(t * 256 + h * LANES, LANES)] = jnp.where(left, one, two)[:OWN]


def shards(panels, blocks, cols):
    count = lax.axis_size("node")
    before = lax.ppermute(panels[:, -BLOCK:], "node", [(i, i + 1) for i in range(count - 1)])
    after = lax.ppermute(panels[:, :BLOCK], "node", [(i + 1, i) for i in range(count - 1)])
    wide = jnp.concatenate([panels, before, after], axis=1)
    gathered = lax.all_gather(wide, "mode", axis=0, tiled=False)
    own, every = mode_tables()
    vmem = pl.BlockSpec(memory_space=pltpu.VMEM)
    return pl.pallas_call(
        kernel,
        out_shape=jax.ShapeDtypeStruct(panels.shape, jnp.float32),
        in_specs=[pl.BlockSpec(memory_space=pltpu.SMEM)] + [vmem] * 5,
        out_specs=vmem,
        scratch_shapes=[
            pltpu.VMEM((GROUPS * STEP, WIDTH), jnp.float32),
            pltpu.VMEM((2 * VARS * PAD, GROUPS * STEP), jnp.bfloat16),
            pltpu.VMEM((MAT, SLOTS, PAD, LANES), jnp.bfloat16),
            pltpu.VMEM((MAT, SLOTS, PAD, LANES), jnp.bfloat16),
            pltpu.VMEM((2, 8 * PAD, PAIRS * LANES), jnp.bfloat16),
            pltpu.VMEM((8, LANES), jnp.float32),
        ],
        compiler_params=pltpu.CompilerParams(vmem_limit_bytes=32 << 20),
        cost_estimate=pl.CostEstimate(flops=600_000_000, bytes_accessed=6_000_000, transcendentals=0),
    )(cols, jnp.asarray(own), jnp.asarray(every), wide, gathered, blocks.reshape(DEPTH, ROWS * BLOCK))


def solution(mesh):
    return jax.shard_map(
        shards,
        mesh=mesh,
        in_specs=(P("mode", "node"), P(None, None, None, "node"), P(None, None, "node")),
        out_specs=P("mode", "node"),
        check_vma=False,
    )
```

```python
import functools

import jax
import jax.numpy as jnp
import numpy as np
from jax import lax
from jax.experimental import pallas as pl
from jax.experimental.pallas import tpu as pltpu
from jax.sharding import PartitionSpec as P

MAT = 11
VARS = MAT - 1
MODES = 288
BLOCK = 64
NNZ = 3
DEPTH = MAT * NNZ * BLOCK
GROUPS = 16
OWN = MODES // GROUPS
ROWS = 8
NODES = ROWS * BLOCK
SLOTS = ROWS + 1
PAD = 32
KINDS = 16
STEP = 24
LANES = 128
PAIRS = 17
TWOS = 6
CUTS = ((0, 512), (512, 512), (1024, 512), (1536, 576))


def counts(mode, entry):
    singles, pairs, triples, at_pair, at_triple = VARS + 1, 0, 0, [], []
    for v in range(VARS):
        at_pair.append(pairs)
        at_triple.append(triples)
        pairs += VARS - v
        triples += (VARS - v) * (VARS - v + 1) // 2

    def found(value, starts):
        run, start = jnp.zeros_like(value), jnp.zeros_like(value)
        for v in range(1, VARS):
            inside = value >= starts[v]
            run, start = jnp.where(inside, v, run), jnp.where(inside, starts[v], start)
        return run, start

    third = mode - (singles + pairs)
    top, start = found(third, at_triple)
    offset = jnp.zeros_like(mode)
    for v in range(1, VARS):
        offset = jnp.where(top == v, at_pair[v], offset)
    is_three, is_two = third >= 0, mode >= singles
    two = jnp.where(is_three, third - start + offset, mode - singles)
    high, start = found(two, at_pair)
    low = jnp.where(is_two, two - start + high, mode - 1)
    count = (low == entry).astype(jnp.int32)
    count = count + ((high == entry) & is_two).astype(jnp.int32) + ((top == entry) & is_three).astype(jnp.int32)
    return jnp.where(mode < singles + pairs + triples, count, 100).astype(jnp.float32)


def split(value):
    high = value.astype(jnp.bfloat16)
    return high, (value - high.astype(jnp.float32)).astype(jnp.bfloat16)


def twice(value, half, left):
    turned = pltpu.roll(value, BLOCK, 1)
    return jnp.where(left, value, turned) if half == 0 else jnp.where(left, turned, value)


def lefts(rows):
    return lax.broadcasted_iota(jnp.int32, (rows, LANES), 1) < BLOCK


def mix(gathered_ref, mixed_hi, mixed_lo, across, beside, panel, coup, edge):
    group = lax.axis_index("mode")
    even = lax.rem(lax.axis_index("node"), 2) == 0
    left = lefts(PAD)

    for g in range(GROUPS):
        rows = jnp.concatenate([gathered_ref[g], jnp.zeros((STEP - OWN, NODES), jnp.float32)], axis=0)
        panel[pl.ds(g * STEP, STEP), :] = rows

    lane = lax.broadcasted_iota(jnp.int32, (KINDS, GROUPS * STEP), 1)
    mode = jnp.where(lax.rem(lane, STEP) < OWN, lane // STEP * OWN + lax.rem(lane, STEP), MODES)
    every = counts(mode, lax.broadcasted_iota(jnp.int32, mode.shape, 0))
    row = lax.broadcasted_iota(jnp.int32, (PAD, LANES), 0)
    mode = jnp.where(row < OWN, group * OWN + row, MODES)
    own = counts(mode, lax.broadcasted_iota(jnp.int32, mode.shape, 1))
    gaps = [own[:, p : p + 1] - every[p : p + 1, :] for p in range(VARS)]
    apart = functools.reduce(lambda a, b: a + b, [g * g for g in gaps])
    adjacent = apart == 1.0
    for p in range(VARS):
        top = jnp.maximum(own[:, p : p + 1], every[p : p + 1, :])
        root = jnp.where(top == 1.0, 1.0, jnp.where(top == 2.0, np.float32(2.0**0.5), np.float32(3.0**0.5)))
        c_hi, c_lo = split(jnp.where(adjacent & (gaps[p] != 0.0), root, 0.0))
        coup[pl.ds(p * PAD, PAD), :] = c_hi
        coup[pl.ds((VARS + p) * PAD, PAD), :] = c_lo

    def keep(i, c, value):
        for half in range(2):
            hi, lo = split(twice(value, half, left))
            mixed_hi[i, 2 * c + half] = hi
            mixed_lo[i, 2 * c + half] = lo
        if c == 0:
            edge[0, i] = value[:STEP]
        if c == NODES // LANES - 1:
            edge[1, i] = value[:STEP]

    valid = own[:, 0:1] < 50.0
    for c in range(NODES // LANES):
        rows = gathered_ref[group, :, c * LANES : (c + 1) * LANES]
        mine = jnp.concatenate([rows, jnp.zeros((PAD - OWN, LANES), jnp.float32)], axis=0)
        keep(0, c, jnp.where(valid, mine, 0.0))
    half = VARS * PAD
    for c0 in range(0, NODES, 256):
        p_hi, p_lo = split(panel[:, c0 : c0 + 256])
        both = jnp.dot(coup[...], p_hi, preferred_element_type=jnp.float32)
        mixed = both[:half] + both[half:] + jnp.dot(coup[:half], p_lo, preferred_element_type=jnp.float32)
        for p in range(VARS):
            for c in range(2):
                keep(p + 1, c0 // LANES + c, mixed[p * PAD : (p + 1) * PAD, c * LANES : (c + 1) * LANES])
    none = jnp.zeros((PAD, LANES), jnp.bfloat16)
    for i in range(MAT):
        mixed_hi[i, ROWS] = none
        mixed_lo[i, ROWS] = none
    near = lefts(STEP)
    for q in range(TWOS):
        a = 2 * q
        b = min(a + 1, MAT - 1)
        head = jnp.where(near, edge[0, a], pltpu.roll(edge[0, b], BLOCK, 1))
        tail = jnp.where(near, pltpu.roll(edge[1, a], BLOCK, 1), edge[1, b])
        across[q] = jnp.where(even, head, tail)
        beside[q] = jnp.where(even, tail, head)


def inner(cols_ref, mixed_hi, mixed_lo, blocks_hbm, part_ref, end_hi, end_lo, lhs, blocks, sems):
    first = lax.axis_index("node") * ROWS
    copies = [
        pltpu.make_async_copy(blocks_hbm.at[pl.ds(k0, kw)], blocks.at[pl.ds(k0, kw)], sems.at[j])
        for j, (k0, kw) in enumerate(CUTS)
    ]
    for copy in copies:
        copy.start()
    left = lefts(PAD)

    def slot(n, r):
        i, s = divmod(n, NNZ)
        rel = cols_ref[s, r, i] - first
        return i, jnp.where((rel < 0) | (rel >= ROWS), ROWS, rel)

    for r in range(ROWS):
        for q in range(PAIRS):
            at = pl.ds(q * LANES, LANES)
            i, a = slot(2 * q, r)
            hi, lo = mixed_hi[i, a], mixed_lo[i, a]
            if 2 * q + 1 < MAT * NNZ:
                i, b = slot(2 * q + 1, r)
                hi = jnp.where(left, hi, mixed_hi[i, b])
                lo = jnp.where(left, lo, mixed_lo[i, b])
            lhs[r // 4, pl.ds((r % 4) * PAD, PAD), at] = hi
            lhs[r // 4, pl.ds((4 + r % 4) * PAD, PAD), at] = lo

    totals = [None, None]
    for copy, (k0, kw) in zip(copies, CUTS):
        copy.wait()
        for t in range(2):
            w_hi, w_lo = split(blocks[pl.ds(k0, kw), pl.ds(t * 256, 256)])
            both = jnp.dot(lhs[t, :, k0 : k0 + kw], w_hi, preferred_element_type=jnp.float32)
            part = both[: 4 * PAD] + both[4 * PAD :]
            part = part + jnp.dot(lhs[t, : 4 * PAD, k0 : k0 + kw], w_lo, preferred_element_type=jnp.float32)
            totals[t] = part if totals[t] is None else totals[t] + part
        ends = jnp.where(lefts(kw), blocks[pl.ds(k0, kw), pl.ds(0, LANES)], blocks[pl.ds(k0, kw), pl.ds(NODES - LANES, LANES)])
        hi, lo = split(ends)
        end_hi[pl.ds(k0, kw), :] = hi
        end_lo[pl.ds(k0, kw), :] = lo
    for t in range(2):
        for h in range(2):
            cut = totals[t][:, h * LANES : (h + 1) * LANES]
            one, two = cut[(2 * h) * PAD : (2 * h + 1) * PAD], cut[(2 * h + 1) * PAD : (2 * h + 2) * PAD]
            part_ref[:, pl.ds(t * 256 + h * LANES, LANES)] = jnp.where(left, one, two)[:OWN]


def outer(cols_ref, across_ref, beside_ref, end_hi, end_lo, part_ref, out_ref, lhs):
    node = lax.axis_index("node")
    first = node * ROWS
    even = lax.rem(node, 2) == 0
    near = lefts(STEP)
    fill = jnp.zeros((PAD - STEP, LANES), jnp.float32)
    for side, (r, want) in enumerate(((0, first - 1), (ROWS - 1, first + ROWS))):
        even_ref, odd_ref = (across_ref, beside_ref) if side == 0 else (beside_ref, across_ref)
        packed = [jnp.where(even, even_ref[q], odd_ref[q]) for q in range(TWOS)]
        both = [twice(packed[i // 2], i % 2, near) for i in range(MAT)]
        for q in range(PAIRS):
            i, s = divmod(2 * q, NNZ)
            value = jnp.where(cols_ref[s, r, i] == want, both[i], 0.0)
            if 2 * q + 1 < MAT * NNZ:
                i, s = divmod(2 * q + 1, NNZ)
                value = jnp.where(near, value, jnp.where(cols_ref[s, r, i] == want, both[i], 0.0))
            hi, lo = split(jnp.concatenate([value, fill], axis=0))
            lhs[pl.ds(side * PAD, PAD), pl.ds(q * LANES, LANES)] = hi
            lhs[pl.ds((2 + side) * PAD, PAD), pl.ds(q * LANES, LANES)] = lo
    twos = jnp.dot(lhs[:, :DEPTH], end_hi[...], preferred_element_type=jnp.float32)
    total = twos[: 2 * PAD] + twos[2 * PAD :]
    total = total + jnp.dot(lhs[: 2 * PAD, :DEPTH], end_lo[...], preferred_element_type=jnp.float32)
    left = lefts(OWN)
    out_ref[...] = part_ref[...]
    out_ref[:, :LANES] = part_ref[:, :LANES] + jnp.where(left, total[:OWN], 0.0)
    out_ref[:, NODES - LANES :] = part_ref[:, NODES - LANES :] + jnp.where(left, 0.0, total[PAD : PAD + OWN])


def shards(panels, blocks, cols):
    count = lax.axis_size("node")
    gathered = lax.all_gather(panels, "mode", axis=0, tiled=False)
    cols = cols.transpose(1, 2, 0)
    vmem = pl.BlockSpec(memory_space=pltpu.VMEM)
    smem = pl.BlockSpec(memory_space=pltpu.SMEM)
    hbm = pl.BlockSpec(memory_space=pltpu.MemorySpace.HBM)
    f32, bf16 = jnp.float32, jnp.bfloat16
    params = pltpu.CompilerParams(vmem_limit_bytes=50 << 20)
    mixed = jax.ShapeDtypeStruct((MAT, SLOTS, PAD, LANES), bf16)
    edge = jax.ShapeDtypeStruct((TWOS, STEP, LANES), f32)
    mixed_hi, mixed_lo, across, beside = pl.pallas_call(
        mix,
        out_shape=(mixed, mixed, edge, edge),
        in_specs=[vmem],
        out_specs=(vmem,) * 4,
        scratch_shapes=[
            pltpu.VMEM((GROUPS * STEP, NODES), f32),
            pltpu.VMEM((2 * VARS * PAD, GROUPS * STEP), bf16),
            pltpu.VMEM((2, MAT, STEP, LANES), f32),
        ],
        compiler_params=params,
        cost_estimate=pl.CostEstimate(flops=400_000_000, bytes_accessed=2_000_000, transcendentals=0),
    )(gathered)
    steps = [(i, i + 1) for i in range(1, count - 1, 2)]
    across = lax.ppermute(across, "node", steps + [(b, a) for a, b in steps])
    beside = lax.ppermute(beside, "node", [(i, i ^ 1) for i in range(count)])
    end = jax.ShapeDtypeStruct((DEPTH, LANES), bf16)
    part, end_hi, end_lo = pl.pallas_call(
        inner,
        out_shape=(jax.ShapeDtypeStruct(panels.shape, f32), end, end),
        in_specs=[smem, vmem, vmem, hbm],
        out_specs=(vmem,) * 3,
        scratch_shapes=[
            pltpu.VMEM((2, 8 * PAD, PAIRS * LANES), bf16),
            pltpu.VMEM((DEPTH, NODES), f32),
            pltpu.SemaphoreType.DMA((len(CUTS),)),
        ],
        compiler_params=params,
        cost_estimate=pl.CostEstimate(flops=900_000_000, bytes_accessed=8_000_000, transcendentals=0),
    )(cols, mixed_hi, mixed_lo, blocks.reshape(DEPTH, NODES))
    return pl.pallas_call(
        outer,
        out_shape=jax.ShapeDtypeStruct(panels.shape, f32),
        in_specs=[smem] + [vmem] * 5,
        out_specs=vmem,
        scratch_shapes=[pltpu.VMEM((4 * PAD, PAIRS * LANES), bf16)],
        compiler_params=params,
        cost_estimate=pl.CostEstimate(flops=100_000_000, bytes_accessed=1_500_000, transcendentals=0),
    )(cols, across, beside, end_hi, end_lo, part)


def solution(mesh):
    return jax.shard_map(
        shards,
        mesh=mesh,
        in_specs=(P("mode", "node"), P(None, None, None, "node"), P(None, None, "node")),
        out_specs=P("mode", "node"),
        check_vma=False,
    )
```

```python
import functools

import jax
import jax.numpy as jnp
import numpy as np
from jax import lax
from jax.experimental import pallas as pl
from jax.experimental.pallas import tpu as pltpu
from jax.sharding import PartitionSpec as P

MAT = 11
VARS = MAT - 1
MODES = 288
BLOCK = 64
NNZ = 3
DEPTH = MAT * NNZ * BLOCK
GROUPS = 16
OWN = MODES // GROUPS
ROWS = 8
NODES = ROWS * BLOCK
SLOTS = ROWS + 2
PAD = 32
KINDS = 16
STEP = 24
LANES = 128
PAIRS = 17
TWOS = 6
CUTS = ((0, 256), (256, 256), (512, 256), (768, 256), (1024, 256), (1280, 256), (1536, 256), (1792, 256), (2048, 64))


def counts(mode, entry):
    singles, pairs, triples, at_pair, at_triple = VARS + 1, 0, 0, [], []
    for v in range(VARS):
        at_pair.append(pairs)
        at_triple.append(triples)
        pairs += VARS - v
        triples += (VARS - v) * (VARS - v + 1) // 2

    def found(value, starts):
        run, start = jnp.zeros_like(value), jnp.zeros_like(value)
        for v in range(1, VARS):
            inside = value >= starts[v]
            run, start = jnp.where(inside, v, run), jnp.where(inside, starts[v], start)
        return run, start

    third = mode - (singles + pairs)
    top, start = found(third, at_triple)
    offset = jnp.zeros_like(mode)
    for v in range(1, VARS):
        offset = jnp.where(top == v, at_pair[v], offset)
    is_three, is_two = third >= 0, mode >= singles
    two = jnp.where(is_three, third - start + offset, mode - singles)
    high, start = found(two, at_pair)
    low = jnp.where(is_two, two - start + high, mode - 1)
    count = (low == entry).astype(jnp.int32)
    count = count + ((high == entry) & is_two).astype(jnp.int32) + ((top == entry) & is_three).astype(jnp.int32)
    return jnp.where(mode < singles + pairs + triples, count, 100).astype(jnp.float32)


def split(value):
    high = value.astype(jnp.bfloat16)
    return high, (value - high.astype(jnp.float32)).astype(jnp.bfloat16)


def twice(value, half, left):
    turned = pltpu.roll(value, BLOCK, 1)
    return jnp.where(left, value, turned) if half == 0 else jnp.where(left, turned, value)


def lefts(rows):
    return lax.broadcasted_iota(jnp.int32, (rows, LANES), 1) < BLOCK


def mix(gathered_ref, mixed_hi, mixed_lo, across, beside, panel, coup, edge):
    group = lax.axis_index("mode")
    even = lax.rem(lax.axis_index("node"), 2) == 0
    near = lefts(STEP)

    for g in range(GROUPS):
        rows = jnp.concatenate([gathered_ref[g], jnp.zeros((STEP - OWN, NODES), jnp.float32)], axis=0)
        panel[pl.ds(g * STEP, STEP), :] = rows

    lane = lax.broadcasted_iota(jnp.int32, (KINDS, GROUPS * STEP), 1)
    mode = jnp.where(lax.rem(lane, STEP) < OWN, lane // STEP * OWN + lax.rem(lane, STEP), MODES)
    every = counts(mode, lax.broadcasted_iota(jnp.int32, mode.shape, 0))
    row = lax.broadcasted_iota(jnp.int32, (STEP, LANES), 0)
    mode = jnp.where(row < OWN, group * OWN + row, MODES)
    own = counts(mode, lax.broadcasted_iota(jnp.int32, mode.shape, 1))
    gaps = [own[:, p : p + 1] - every[p : p + 1, :] for p in range(VARS)]
    apart = functools.reduce(lambda a, b: a + b, [g * g for g in gaps])
    adjacent = apart == 1.0
    for p in range(VARS):
        top = jnp.maximum(own[:, p : p + 1], every[p : p + 1, :])
        root = jnp.where(top == 1.0, 1.0, jnp.where(top == 2.0, np.float32(2.0**0.5), np.float32(3.0**0.5)))
        coup[pl.ds(p * STEP, STEP), :] = jnp.where(adjacent & (gaps[p] != 0.0), root, 0.0)

    def keep(i, c, value):
        for half in range(2):
            hi, lo = split(twice(value, half, near))
            mixed_hi[i, 2 * c + half + 1, :STEP] = hi
            mixed_lo[i, 2 * c + half + 1, :STEP] = lo
        if c == 0:
            edge[0, i] = value
        if c == NODES // LANES - 1:
            edge[1, i] = value

    valid = own[:, 0:1] < 50.0
    for c in range(NODES // LANES):
        rows = gathered_ref[group, :, c * LANES : (c + 1) * LANES]
        mine = jnp.concatenate([rows, jnp.zeros((STEP - OWN, LANES), jnp.float32)], axis=0)
        keep(0, c, jnp.where(valid, mine, 0.0))
    c_hi, c_lo = split(coup[...])
    for c0 in range(0, NODES, 256):
        p_hi, p_lo = split(panel[:, c0 : c0 + 256])
        mixed = jnp.dot(c_hi, p_hi, preferred_element_type=jnp.float32)
        mixed = mixed + jnp.dot(c_lo, p_hi, preferred_element_type=jnp.float32)
        mixed = mixed + jnp.dot(c_hi, p_lo, preferred_element_type=jnp.float32)
        for p in range(VARS):
            for c in range(2):
                keep(p + 1, c0 // LANES + c, mixed[p * STEP : (p + 1) * STEP, c * LANES : (c + 1) * LANES])
    none = jnp.zeros((PAD, LANES), jnp.bfloat16)
    for i in range(MAT):
        for none_at in (0, ROWS + 1):
            mixed_hi[i, none_at] = none
            mixed_lo[i, none_at] = none
    for q in range(TWOS):
        a = 2 * q
        b = min(a + 1, MAT - 1)
        head = jnp.where(near, edge[0, a], pltpu.roll(edge[0, b], BLOCK, 1))
        tail = jnp.where(near, pltpu.roll(edge[1, a], BLOCK, 1), edge[1, b])
        across[q] = jnp.where(even, head, tail)
        beside[q] = jnp.where(even, tail, head)


def inner(cols_ref, mixed_hi, mixed_lo, blocks, part_ref, end_hi, end_lo, mask_ref, lhs):
    first = lax.axis_index("node") * ROWS
    before = first - 1
    left = lefts(PAD)

    def slot(n, r):
        i, s = divmod(n, NNZ)
        return i, cols_ref[s, r, i] - before

    for t in range(2):
        for r in range(4 * t, 4 * t + 4):
            for q in range(PAIRS):
                at = pl.ds(q * LANES, LANES)
                i, a = slot(2 * q, r)
                hi, lo = mixed_hi[i, a], mixed_lo[i, a]
                if 2 * q + 1 < MAT * NNZ:
                    i, b = slot(2 * q + 1, r)
                    hi = jnp.where(left, hi, mixed_hi[i, b])
                    lo = jnp.where(left, lo, mixed_lo[i, b])
                lhs[t, pl.ds((r % 4) * PAD, PAD), at] = hi
                lhs[t, pl.ds((4 + r % 4) * PAD, PAD), at] = lo
    for t in range(2):
        total = None
        for k0, kw in CUTS:
            w_hi, w_lo = split(blocks[pl.ds(k0, kw), pl.ds(t * 256, 256)])
            both = jnp.dot(lhs[t, :, k0 : k0 + kw], w_hi, preferred_element_type=jnp.float32)
            part = both[: 4 * PAD] + both[4 * PAD :]
            part = part + jnp.dot(lhs[t, : 4 * PAD, k0 : k0 + kw], w_lo, preferred_element_type=jnp.float32)
            total = part if total is None else total + part
            if t == 0:
                end_hi[pl.ds(k0, kw), :BLOCK] = w_hi[:, :BLOCK]
                end_lo[pl.ds(k0, kw), :BLOCK] = w_lo[:, :BLOCK]
            else:
                end_hi[pl.ds(k0, kw), BLOCK:] = w_hi[:, 256 - BLOCK :]
                end_lo[pl.ds(k0, kw), BLOCK:] = w_lo[:, 256 - BLOCK :]
        for h in range(2):
            cut = total[:, h * LANES : (h + 1) * LANES]
            one, two = cut[(2 * h) * PAD : (2 * h + 1) * PAD], cut[(2 * h + 1) * PAD : (2 * h + 2) * PAD]
            part_ref[:, pl.ds(t * 256 + h * LANES, LANES)] = jnp.where(left, one, two)[:OWN]

    few = lefts(8)
    for side, (r, want) in enumerate(((0, first - 1), (ROWS - 1, first + ROWS))):
        for q in range(PAIRS):
            i, s = divmod(2 * q, NNZ)
            j, u = divmod(min(2 * q + 1, MAT * NNZ - 1), NNZ)
            a = (cols_ref[s, r, i] == want).astype(jnp.float32)
            b = (cols_ref[u, r, j] == want).astype(jnp.float32)
            mask_ref[side, :, pl.ds(q * LANES, LANES)] = jnp.where(few, a, b)


def outer(beside_ref, across_ref, end_hi, end_lo, mask_ref, part_ref, out_ref, lhs):
    even = lax.rem(lax.axis_index("node"), 2) == 0
    near = lefts(STEP)
    for side in range(2):
        even_ref, odd_ref = (across_ref, beside_ref.at[0]) if side == 0 else (beside_ref.at[1], across_ref)
        both = []
        for k in range(TWOS):
            packed = jnp.where(even, even_ref[k], odd_ref[k])
            turned = pltpu.roll(packed, BLOCK, 1)
            first, second = jnp.where(near, packed, turned), jnp.where(near, turned, packed)
            both += [first, second]
        for q in range(PAIRS):
            i, j = 2 * q // NNZ, min(2 * q + 1, MAT * NNZ - 1) // NNZ
            value = both[i] if i == j else jnp.where(near, both[i], both[j])
            mask = mask_ref[side, :, pl.ds(q * LANES, LANES)]
            value = jnp.where(jnp.concatenate([mask] * (STEP // 8), axis=0) != 0.0, value, 0.0)
            hi, lo = split(value)
            lhs[pl.ds(side * PAD, STEP), pl.ds(q * LANES, LANES)] = hi
            lhs[pl.ds((2 + side) * PAD, STEP), pl.ds(q * LANES, LANES)] = lo
    twos = jnp.dot(lhs[:, :DEPTH], end_hi[...], preferred_element_type=jnp.float32)
    total = twos[: 2 * PAD] + twos[2 * PAD :]
    total = total + jnp.dot(lhs[: 2 * PAD, :DEPTH], end_lo[...], preferred_element_type=jnp.float32)
    left = lefts(OWN)
    out_ref[...] = part_ref[...]
    out_ref[:, :LANES] = part_ref[:, :LANES] + jnp.where(left, total[:OWN], 0.0)
    out_ref[:, NODES - LANES :] = part_ref[:, NODES - LANES :] + jnp.where(left, 0.0, total[PAD : PAD + OWN])


def shards(panels, blocks, cols):
    count = lax.axis_size("node")
    gathered = lax.all_gather(panels, "mode", axis=0, tiled=False)
    cols = cols.transpose(1, 2, 0)
    vmem = pl.BlockSpec(memory_space=pltpu.VMEM)
    smem = pl.BlockSpec(memory_space=pltpu.SMEM)
    f32, bf16 = jnp.float32, jnp.bfloat16
    params = pltpu.CompilerParams(vmem_limit_bytes=24 << 20)
    mixed = jax.ShapeDtypeStruct((MAT, SLOTS, PAD, LANES), bf16)
    edge = jax.ShapeDtypeStruct((TWOS, STEP, LANES), f32)
    mixed_hi, mixed_lo, across, beside = pl.pallas_call(
        mix,
        out_shape=(mixed, mixed, edge, edge),
        in_specs=[vmem],
        out_specs=(vmem,) * 4,
        scratch_shapes=[
            pltpu.VMEM((GROUPS * STEP, NODES), f32),
            pltpu.VMEM((VARS * STEP, GROUPS * STEP), f32),
            pltpu.VMEM((2, MAT, STEP, LANES), f32),
        ],
        compiler_params=params,
        cost_estimate=pl.CostEstimate(flops=4_000_000_000, bytes_accessed=20_000_000, transcendentals=0),
    )(gathered)
    steps = [(i, i + 1) for i in range(1, count - 1, 2)]
    across = lax.ppermute(across, "node", steps + [(b, a) for a, b in steps])
    beside = lax.all_gather(beside, "node", axis=0, axis_index_groups=[[i, i + 1] for i in range(0, count, 2)])
    end = jax.ShapeDtypeStruct((DEPTH, LANES), bf16)
    mask = jax.ShapeDtypeStruct((2, 8, PAIRS * LANES), f32)
    part, end_hi, end_lo, mask = pl.pallas_call(
        inner,
        out_shape=(jax.ShapeDtypeStruct(panels.shape, f32), end, end, mask),
        in_specs=[smem, vmem, vmem, vmem],
        out_specs=(vmem,) * 4,
        scratch_shapes=[
            pltpu.VMEM((2, 8 * PAD, PAIRS * LANES), bf16),
        ],
        compiler_params=params,
        cost_estimate=pl.CostEstimate(flops=900_000_000, bytes_accessed=8_000_000, transcendentals=0),
    )(cols, mixed_hi, mixed_lo, blocks.reshape(DEPTH, NODES))
    return pl.pallas_call(
        outer,
        out_shape=jax.ShapeDtypeStruct(panels.shape, f32),
        in_specs=[vmem] * 6,
        out_specs=vmem,
        scratch_shapes=[pltpu.VMEM((4 * PAD, PAIRS * LANES), bf16)],
        compiler_params=params,
        cost_estimate=pl.CostEstimate(flops=100_000_000, bytes_accessed=1_500_000, transcendentals=0),
    )(beside, across, end_hi, end_lo, mask, part)


def solution(mesh):
    return jax.shard_map(
        shards,
        mesh=mesh,
        in_specs=(P("mode", "node"), P(None, None, None, "node"), P(None, None, "node")),
        out_specs=P("mode", "node"),
        check_vma=False,
    )
```
